32 devices in a mesh: grp: 2 (over y), chan: 4 (over z), col: 2 (over x), sub: 2 (over core).
Axes of the slice: x: 2, y: 2, z: 4, core: 2. Of those that a mesh axis runs over, the one named last changes fastest.
Arguments:
- generator: float32 [8, 1024, 1024], P(('grp', 'chan'), 'sub', 'col'), parts along dimension 0, may hold values from -2 to 2
- interaction: float32 [8, 1024, 1024], P(('grp', 'chan'), 'sub', 'col'), parts along dimension 0, may hold values from -2 to 2
- occupations: int32 [160], replicated, may hold values 0 or 1
- pair_orbits: int32 [4, 2, 1024], P('chan'), may hold values from 0 to 159
- cross_orbits: int32 [4, 2, 1024], P('chan'), may hold values from 0 to 159
- pair_sizes: int32 [4], P('chan'), may hold values from 256 to 1024
- cross_sizes: int32 [4], P('chan'), may hold values from 256 to 1024
- cross_target: int32 [4, 32, 8], P('chan', 'sub', 'col'), may hold values from 0 to 255, as said below
Outputs:
- commutator: float32 [8, 1024, 1024], P(('grp', 'chan'), 'sub', 'col'), parts along dimension 0
The draws below stay inside these ranges and needn't reach their ends.
There are 2 independent parts, one for each index of `grp`. The reference program is written for one: setup_inputs(seed, part) draws one part's arguments, and reference() takes and returns one part's arrays. A program takes and returns all parts, laid end to end along the dimension named above; an argument that names none is the same for every part. Nothing has to cross between parts.
Inputs may be any that keep to these rules, and one draw needn't show every extreme that they name: `cross_target`: each value is d * 64 + j: the tile goes to crossed channel d as tile j of the block with the same rows and columns as its own (tiles numbered row by row within the block). Every tile of every crossed channel receives exactly one tile. At most 32 tiles of one block go to one crossed channel, and in every block some crossed channel receives exactly 32.
All inputs are finite; a program needn't handle non-finite values.
Results may differ from the reference program's by a relative error of at most 0.0003.
Values sent between devices are 32-bit elements; how exact they have to be, the bound alone decides.
A program may use at most 64 MiB of HBM per device.

```python
import jax
import jax.numpy as jnp
from jax import lax

ORBITALS = 160
M = 1024
TR = 32
TC = 128
CHANNELS = 4
TILES_DEV = 64
CAP = 32
N_COL = 2
N_SUB = 2


def shuffle_slots(slot_key):
    return jax.random.permutation(slot_key, TILES_DEV).astype(jnp.int32)


def one_block(key, block_index):
    block_key = jax.random.fold_in(key, block_index + 11)
    first_key, order_key, sender_key, taker_key = jax.random.split(block_key, 4)
    fullest = jax.random.randint(first_key, (), 0, CHANNELS)
    offsets = jnp.tile(jnp.arange(CHANNELS, dtype=jnp.int32), CAP)
    ranking = jax.random.permutation(order_key, CHANNELS * CAP).astype(jnp.int32)
    ranking = jnp.where(offsets == fullest, ranking - CHANNELS * CAP, ranking)
    shifts = offsets[jnp.argsort(ranking, stable=True)][:TILES_DEV]
    senders = jax.vmap(shuffle_slots)(jax.random.split(sender_key, CHANNELS))
    takers = jax.vmap(shuffle_slots)(jax.random.split(taker_key, CHANNELS))
    sources = jnp.arange(CHANNELS, dtype=jnp.int32)[:, None]
    owners = (sources + shifts[None, :]) % CHANNELS
    taken = takers[owners, jnp.arange(TILES_DEV, dtype=jnp.int32)[None, :]]
    values = owners * TILES_DEV + taken
    return jnp.take_along_axis(values, jnp.argsort(senders, axis=1, stable=True), axis=1)


def partial_block(key):

    def single_block(block_index):
        return one_block(key, block_index)
    return single_block


def draw_cross_target(key, part):
    block_rows = M // N_SUB // TR
    block_cols = M // N_COL // TC
    indices = jnp.arange(N_SUB * N_COL, dtype=jnp.int32)
    blocks = jax.vmap(partial_block(key))(indices)
    shaped = blocks.reshape(N_SUB, N_COL, CHANNELS, block_rows, block_cols)
    return shaped.transpose(2, 0, 3, 1, 4).reshape(CHANNELS, M // TR, M // TC).astype(jnp.int32)


def plant(values, own_key, least, largest):
    shape = values.shape
    index_at = [jax.random.randint(jax.random.fold_in(own_key, axis), (), 0, shape[axis]) for axis in range(len(shape))]
    values = values.at[tuple(index_at)].set(least)
    longest = shape.index(max(shape))
    index_at[longest] = (index_at[longest] + 1) % shape[longest]
    return values.at[tuple(index_at)].set(largest)


def block_scale(rng, extent, pieces, low, top_value):
    factor_of, own = 1.0, jax.random.fold_in(rng, 6)
    for axis_at, parts in pieces:
        draws = jnp.exp(jax.random.uniform(jax.random.fold_in(own, axis_at), (parts,), jnp.float32, low / len(pieces), top_value / len(pieces)))
        factor_of = factor_of * jnp.repeat(draws, extent[axis_at] // parts).reshape([-1 if axis == axis_at else 1 for axis in range(len(extent))])
    return factor_of


def gaussian(key, extent, width, bound, pieces=(), kind=jnp.bfloat16):
    loudness = block_scale(key, extent, pieces, -0.22, 0.18) if pieces else 1.0
    result = jax.random.normal(key, extent, jnp.float32) * width * loudness
    return jnp.minimum(jnp.maximum(result, -bound), bound).astype(kind)


def setup_inputs(seed: int = 0, part: int = 0) -> dict:
    streams_of = jax.random.split(jax.random.key(seed), 9)
    part_keys = jax.random.split(jax.random.fold_in(streams_of[8], part), 9)
    generator = gaussian(part_keys[0], (CHANNELS, M, M), 0.14, 2.0, ((0, 4), (1, 2), (2, 2)), jnp.float32)
    interaction = gaussian(part_keys[1], (CHANNELS, M, M), 0.14, 2.0, ((0, 4), (1, 2), (2, 2)), jnp.float32)
    occupations = plant((jax.random.randint(streams_of[2], (ORBITALS,), 0, 4) < 1).astype(jnp.int32), jax.random.fold_in(streams_of[2], 1), 0, 1)
    pair_orbits = plant(jax.random.randint(streams_of[3], (CHANNELS, 2, M), 0, ORBITALS), jax.random.fold_in(streams_of[3], 1), 0, ORBITALS - 1).astype(jnp.int32)
    cross_orbits = plant(jax.random.randint(streams_of[4], (CHANNELS, 2, M), 0, ORBITALS), jax.random.fold_in(streams_of[4], 1), 0, ORBITALS - 1).astype(jnp.int32)
    pair_sizes = plant(jax.random.randint(streams_of[5], (CHANNELS,), M // 4, M + 1), jax.random.fold_in(streams_of[5], 1), M // 4, M).astype(jnp.int32)
    cross_sizes = plant(jax.random.randint(streams_of[6], (CHANNELS,), M // 4, M + 1), jax.random.fold_in(streams_of[6], 1), M // 4, M).astype(jnp.int32)
    cross_target = draw_cross_target(jax.random.fold_in(streams_of[8], 71), part)
    return {"generator": generator, "interaction": interaction, "occupations": occupations, "pair_orbits": pair_orbits, "cross_orbits": cross_orbits, "pair_sizes": pair_sizes, "cross_sizes": cross_sizes, "cross_target": cross_target}


def occupancy(orbit_pairs, filled, size_limits, particle):
    first_filled = filled[orbit_pairs[:, 0, :]]
    second_filled = filled[orbit_pairs[:, 1, :]]
    live_pairs = (jnp.arange(M, dtype=jnp.int32)[None, :] < size_limits[:, None]).astype(jnp.float32)
    if particle:
        factor = 1.0 - first_filled - second_filled
    else:
        factor = first_filled - second_filled
    return factor * live_pairs


def bracket(left_side, right_side, weights):
    def single(operands):
        left_block, right_block, weight_row = operands
        forward = jnp.dot(left_block * weight_row[None, :], right_block, precision=lax.Precision.HIGHEST, preferred_element_type=jnp.float32)
        reverse = jnp.dot(right_block * weight_row[None, :], left_block, precision=lax.Precision.HIGHEST, preferred_element_type=jnp.float32)
        return forward - reverse
    return lax.map(single, (left_side, right_side, weights))


def split_tiles(matrices):
    channel_count = matrices.shape[0]
    tiled = matrices.reshape(channel_count, M // TR, TR, M // TC, TC)
    return tiled.transpose(0, 1, 3, 2, 4).reshape(-1, TR, TC)


def join_tiles(tiles, channel_count):
    tiled = tiles.reshape(channel_count, M // TR, M // TC, TR, TC)
    return tiled.transpose(0, 1, 3, 2, 4).reshape(channel_count, M, M)


def destinations(cross_target):
    block_rows = M // N_SUB // TR
    block_cols = M // N_COL // TC
    per_block = block_rows * block_cols
    channel_to = cross_target // per_block
    slot_to = cross_target % per_block
    tile_row = jnp.arange(M // TR, dtype=jnp.int32)[None, :, None]
    tile_col = jnp.arange(M // TC, dtype=jnp.int32)[None, None, :]
    row_to = (tile_row // block_rows) * block_rows + slot_to // block_cols
    col_to = (tile_col // block_cols) * block_cols + slot_to % block_cols
    return ((channel_to * (M // TR) + row_to) * (M // TC) + col_to).reshape(-1).astype(jnp.int32)


def reference(generator, interaction, occupations, pair_orbits, cross_orbits, pair_sizes, cross_sizes, cross_target):
    channel_count = generator.shape[0]
    filled = occupations.astype(jnp.float32)
    live_rows = (jnp.arange(M, dtype=jnp.int32)[None, :] < pair_sizes[:, None]).astype(jnp.float32)
    live_block = live_rows[:, :, None] * live_rows[:, None, :]
    generator_live = generator * live_block
    interaction_live = interaction * live_block
    particle = bracket(generator_live, interaction_live, occupancy(pair_orbits, filled, pair_sizes, True))
    flat_to = destinations(cross_target)
    empty_tiles = jnp.zeros((channel_count * (M // TR) * (M // TC), TR, TC), jnp.float32)
    crossed_generator = join_tiles(empty_tiles.at[flat_to].set(split_tiles(generator_live)), channel_count)
    crossed_interaction = join_tiles(empty_tiles.at[flat_to].set(split_tiles(interaction_live)), channel_count)
    crossed = bracket(crossed_generator, crossed_interaction, occupancy(cross_orbits, filled, cross_sizes, False))
    returned = join_tiles(split_tiles(crossed)[flat_to], channel_count)
    return live_block * (particle - returned)
```

```python
import functools

import jax
import jax.numpy as jnp
from jax import lax
from jax.experimental import pallas as pl
from jax.experimental.pallas import tpu as pltpu
from jax.sharding import PartitionSpec as P

TR = 32
TC = 128
LANES = 128
MESH = pl.DeviceIdType.MESH
VMEM_LIMIT = 60 * 1024 * 1024


def split(value):
    high = value.astype(jnp.bfloat16)
    low = (value - high.astype(jnp.float32)).astype(jnp.bfloat16)
    return high, low


def rank_order(count):
    far = sorted(range(1, count), key=lambda d: (-min(d, count - d), -d))
    return far


def kernel(
    sizes,
    gen_ref,
    int_ref,
    pair_orb_ref,
    cross_orb_ref,
    filled_ref,
    size_ref,
    pack_ref,
    ret_ref,
    meta_ref,
    out_ref,
    tiled_g,
    tiled_i,
    send_g,
    send_i,
    raw_g,
    raw_i,
    rawx_g,
    rawx_i,
    raws_g,
    raws_i,
    meta_own,
    meta_x,
    meta_s,
    smeta_own,
    smeta_x,
    smeta_s,
    left_g_hi,
    left_g_lo,
    left_i_hi,
    left_i_lo,
    right_g_hi,
    right_g_lo,
    right_i_hi,
    right_i_lo,
    product,
    back_send,
    back_recv,
    partx,
    parts,
    particle,
    weights,
    z_send,
    z_recv,
    x_send,
    x_recv,
    s_send,
    s_recv,
    m_send,
    m_recv,
    local_sem,
    b_send,
    b_recv,
    p_send,
    p_recv,
):
    n_chan, n_col, n_sub, height, width, cap, chunk = sizes
    n_chunk = cap // chunk
    rt, ct = height // TR, width // TC
    tiles = rt * ct
    me = lax.axis_index("chan")
    my_col = lax.axis_index("col")
    my_sub = lax.axis_index("sub")

    def at(axis, index, count, step):
        return {axis: lax.rem(index + step, count)}

    def to_chan(step):
        return at("chan", me, n_chan, step)

    def to_col(step):
        return at("col", my_col, n_col, step)

    def to_sub(step):
        return at("sub", my_sub, n_sub, step)

    distances = rank_order(n_chan)

    barrier = pltpu.get_barrier_semaphore()
    for d in range(1, n_chan):
        pl.semaphore_signal(barrier, inc=1, device_id=to_chan(d), device_id_type=MESH)
    for d in range(1, n_col):
        pl.semaphore_signal(barrier, inc=1, device_id=to_col(d), device_id_type=MESH)
    for d in range(1, n_sub):
        pl.semaphore_signal(barrier, inc=1, device_id=to_sub(d), device_id_type=MESH)

    limit = size_ref[0]
    row_in = lax.broadcasted_iota(jnp.int32, (TR, TC), 0) + my_sub * height
    col_in = lax.broadcasted_iota(jnp.int32, (TR, TC), 1) + my_col * width

    def live_of(r, t):
        keep = (row_in + r * TR < limit) & (col_in + t * TC < limit)
        return keep.astype(jnp.float32)

    own_meta = pltpu.make_async_copy(meta_ref.at[me], meta_own.at[me], local_sem.at[0])
    own_meta.start()

    def to_tiles(r, carry):
        rows = pl.ds(pl.multiple_of(r * TR, TR), TR)
        for t in range(ct):
            keep = live_of(r, t)
            cols = pl.ds(t * TC, TC)
            tiled_g[r * ct + t] = gen_ref[rows, cols] * keep
            tiled_i[r * ct + t] = int_ref[rows, cols] * keep
        return carry

    lax.fori_loop(0, rt, to_tiles, 0)

    def pack_one(tiled, sent, raw):
        for d in distances:
            base = lax.rem(me + d, n_chan) * cap

            def put(k, carry, base=base, d=d):
                sent[(d - 1) * cap + k] = tiled[pack_ref[base + k]]
                return carry

            lax.fori_loop(0, cap, put, 0, unroll=min(cap, 4))

        def keep_own(k, carry):
            raw[me * cap + k] = tiled[pack_ref[me * cap + k]]
            return carry

        lax.fori_loop(0, cap, keep_own, 0, unroll=min(cap, 4))

    pack_one(tiled_g, send_g, raw_g)
    pack_one(tiled_i, send_i, raw_i)
    pl.semaphore_wait(barrier, n_chan + n_col + n_sub - 3)

    started = []

    def remote(src, dst, ssem, rsem, device):
        copy = pltpu.make_async_remote_copy(
            src_ref=src,
            dst_ref=dst,
            send_sem=ssem,
            recv_sem=rsem,
            device_id=device,
            device_id_type=MESH,
        )
        copy.start()
        started.append(copy)
        return copy

    meta_copies = [
        remote(
            meta_ref.at[lax.rem(me + d, n_chan)],
            meta_own.at[me],
            m_send.at[d - 1],
            m_recv.at[d - 1],
            to_chan(d),
        )
        for d in distances
    ]
    sent = (send_g, send_i)
    raw = (raw_g, raw_i)
    rawx = (rawx_g, rawx_i)
    raws = (raws_g, raws_i)
    z_copies = {}
    for m in range(2):
        for q in range(n_chunk):
            for d in distances:
                z_copies[m, q, d] = remote(
                    sent[m].at[pl.ds((d - 1) * cap + q * chunk, chunk)],
                    raw[m].at[pl.ds(me * cap + q * chunk, chunk)],
                    z_send.at[m, q, d - 1],
                    z_recv.at[m, q, d - 1],
                    to_chan(d),
                )

    x_copies, s_copies = {}, {}

    def forward(m, q, d):
        source = lax.rem(me + n_chan - d, n_chan)
        rows = pl.ds(source * cap + q * chunk, chunk)
        for e in range(1, n_col):
            x_copies[m, q, d, e] = remote(
                raw[m].at[rows],
                rawx[m].at[e - 1, rows],
                x_send.at[m, q, d, e - 1],
                x_recv.at[m, q, d, e - 1],
                to_col(e),
            )
        for e in range(1, n_sub):
            s_copies[m, q, d, e] = remote(
                raw[m].at[rows],
                raws[m].at[e - 1, rows],
                s_send.at[m, q, d, e - 1],
                s_recv.at[m, q, d, e - 1],
                to_sub(e),
            )

    for m in range(2):
        for q in range(n_chunk):
            forward(m, q, 0)

    states = pair_orb_ref.shape[1]

    def look_up(orbit, found):
        value = filled_ref[orbit]
        pair_found, cross_found = found
        pair_found = pair_found + jnp.where(pair_orb_ref[...] == orbit, value, 0.0)
        cross_found = cross_found + jnp.where(cross_orb_ref[...] == orbit, value, 0.0)
        return pair_found, cross_found

    zero = jnp.zeros((2, states), jnp.float32)
    pair_found, cross_found = lax.fori_loop(0, filled_ref.shape[0], look_up, (zero, zero))
    state_id = lax.broadcasted_iota(jnp.int32, (1, states), 1)
    pair_weight = (1.0 - pair_found[0:1] - pair_found[1:2]) * (state_id < limit).astype(jnp.float32)
    cross_weight = (cross_found[0:1] - cross_found[1:2]) * (state_id < size_ref[1]).astype(
        jnp.float32
    )
    for g in range(states // TC):
        weights[0, g] = jnp.broadcast_to(pair_weight[:, g * TC : (g + 1) * TC], (8, TC))
        weights[1, g] = jnp.broadcast_to(cross_weight[:, g * TC : (g + 1) * TC], (8, TC))

    own_meta.wait()
    for copy in meta_copies:
        copy.wait_recv()
    meta_next = []
    for e in range(1, n_col):
        meta_next.append(
            remote(
                meta_own,
                meta_x.at[e - 1],
                m_send.at[n_chan - 1 + e - 1],
                m_recv.at[n_chan - 1 + e - 1],
                to_col(e),
            )
        )
    for e in range(1, n_sub):
        meta_next.append(
            remote(
                meta_own,
                meta_s.at[e - 1],
                m_send.at[n_chan + n_col - 2 + e - 1],
                m_recv.at[n_chan + n_col - 2 + e - 1],
                to_sub(e),
            )
        )
    for copy in meta_next:
        copy.wait_recv()
    scalar_copies = [
        pltpu.make_async_copy(meta_own, smeta_own, local_sem.at[0]),
        pltpu.make_async_copy(meta_x, smeta_x, local_sem.at[1]),
        pltpu.make_async_copy(meta_s, smeta_s, local_sem.at[2]),
    ]
    for copy in scalar_copies:
        copy.start()
    for copy in scalar_copies:
        copy.wait()

    left = ((left_g_hi, left_g_lo), (left_i_hi, left_i_lo))
    right = ((right_g_hi, right_g_lo), (right_i_hi, right_i_lo))

    def put_left(which, m, block, rows, t, value):
        weight = weights[which, block * ct + t][0:1]
        signed = value * (weight if m == 0 else -weight)
        high, low = split(signed)
        cols = pl.ds(t * TC, TC)
        left[m][0][block, rows, cols] = high
        left[m][1][block, rows, cols] = low

    def put_right(m, block, r, t, value):
        rows = pl.ds(pl.multiple_of(block * height + r * TR, TR), TR)
        high, low = split(value)
        cols = pl.ds(t * TC, TC)
        right[m][0][rows, cols] = high
        right[m][1][rows, cols] = low

    def assemble(m, read_tile, slot_of, in_left, in_right):
        def one_row(r, carry):
            rows = pl.ds(pl.multiple_of(r * TR, TR), TR)
            for t in range(ct):
                j = r * ct + t
                where = slot_of(0, j)
                for source in range(1, n_chan):
                    where = where + slot_of(source, j)
                value = read_tile(where)
                if in_left is not None:
                    put_left(1, m, in_left, rows, t, value)
                if in_right is not None:
                    put_right(m, in_right, r, t, value)
            return carry

        lax.fori_loop(0, rt, one_row, 0)

    def assemble_own(m):
        assemble(
            m, lambda w: raw[m][w], lambda source, j: smeta_own[source, 0, j], my_col, my_sub
        )

    def assemble_sub(m):
        for e in range(1, n_sub):
            assemble(
                m,
                lambda w, e=e: raws[m][e - 1, w],
                lambda source, j, e=e: smeta_s[e - 1, source, 0, j],
                None,
                lax.rem(my_sub + n_sub - e, n_sub),
            )

    def assemble_col(m):
        for e in range(1, n_col):
            assemble(
                m,
                lambda w, e=e: rawx[m][e - 1, w],
                lambda source, j, e=e: smeta_x[e - 1, source, 0, j],
                lax.rem(my_col + n_col - e, n_col),
                None,
            )

    def wait_all(copies, m):
        for key, copy in copies.items():
            if key[0] == m:
                copy.wait_recv()

    def take(m, q):
        for d in distances:
            z_copies[m, q, d].wait_recv()
            forward(m, q, d)

    for q in range(n_chunk):
        take(0, q)
    take(1, 0)
    assemble_own(0)
    if n_chunk > 1:
        take(1, 1)
    wait_all(s_copies, 0)
    assemble_sub(0)
    wait_all(x_copies, 0)
    assemble_col(0)
    for q in range(2, n_chunk):
        take(1, q)

    p_copies = []
    for m, ref in enumerate((gen_ref, int_ref)):
        for e in range(1, n_col):
            p_copies.append(
                remote(
                    ref,
                    partx.at[m, e - 1],
                    p_send.at[m, e - 1],
                    p_recv.at[m, e - 1],
                    to_col(e),
                )
            )
        for e in range(1, n_sub):
            p_copies.append(
                remote(
                    ref,
                    parts.at[m, e - 1],
                    p_send.at[m, n_col - 1 + e - 1],
                    p_recv.at[m, n_col - 1 + e - 1],
                    to_sub(e),
                )
            )
    assemble_own(1)
    wait_all(s_copies, 1)
    assemble_sub(1)
    wait_all(x_copies, 1)
    assemble_col(1)

    tall = min(256, height)
    wide = min(256, width)

    def multiply(write):
        def one(step, carry):
            rows = pl.ds(pl.multiple_of(step * tall, tall), tall)
            for c in range(width // wide):
                cols = pl.ds(c * wide, wide)
                total = None
                for k in range(n_col):
                    depth = pl.ds(k * width, width)
                    for m in range(2):
                        a_hi = left[m][0][k, rows, :]
                        a_lo = left[m][1][k, rows, :]
                        b_hi = right[1 - m][0][depth, cols]
                        b_lo = right[1 - m][1][depth, cols]
                        for a, b in ((a_hi, b_hi), (a_hi, b_lo), (a_lo, b_hi)):
                            term = jnp.dot(a, b, preferred_element_type=jnp.float32)
                            total = term if total is None else total + term
                write(step, rows, c, cols, total)
            return carry

        lax.fori_loop(0, height // tall, one, 0)

    def write_product(step, rows, c, cols, total):
        for r in range(tall // TR):
            for t in range(wide // TC):
                index = (step * (tall // TR) + r) * ct + c * (wide // TC) + t
                product[index] = total[r * TR : (r + 1) * TR, t * TC : (t + 1) * TC]

    multiply(write_product)

    for d in distances:
        target = lax.rem(me + d, n_chan)

        def put_back(k, carry, target=target, d=d):
            back_send[(d - 1) * cap + k] = product[smeta_own[target, 0, tiles + k]]
            return carry

        lax.fori_loop(0, cap, put_back, 0, unroll=min(cap, 4))

    def keep_back(k, carry):
        back_recv[me * cap + k] = product[smeta_own[me, 0, tiles + k]]
        return carry

    lax.fori_loop(0, cap, keep_back, 0, unroll=min(cap, 4))
    back_copies = [
        remote(
            back_send.at[pl.ds((d - 1) * cap, cap)],
            back_recv.at[pl.ds(me * cap, cap)],
            b_send.at[d - 1],
            b_recv.at[d - 1],
            to_chan(d),
        )
        for d in distances
    ]

    def place(m, read, in_left, in_right):
        def one_row(r, carry):
            rows = pl.ds(pl.multiple_of(r * TR, TR), TR)
            for t in range(ct):
                value = read(rows, pl.ds(t * TC, TC))
                if in_left is not None:
                    put_left(0, m, in_left, rows, t, value)
                if in_right is not None:
                    put_right(m, in_right, r, t, value)
            return carry

        lax.fori_loop(0, rt, one_row, 0)

    for m, ref in enumerate((gen_ref, int_ref)):
        place(m, lambda rows, cols, ref=ref: ref[rows, cols], my_col, my_sub)
    for copy in p_copies:
        copy.wait_recv()
    for m in range(2):
        for e in range(1, n_sub):
            place(
                m,
                lambda rows, cols, m=m, e=e: parts[m, e - 1, rows, cols],
                None,
                lax.rem(my_sub + n_sub - e, n_sub),
            )
        for e in range(1, n_col):
            place(
                m,
                lambda rows, cols, m=m, e=e: partx[m, e - 1, rows, cols],
                lax.rem(my_col + n_col - e, n_col),
                None,
            )

    def write_particle(step, rows, c, cols, total):
        particle[rows, cols] = total

    multiply(write_particle)

    for copy in back_copies:
        copy.wait_recv()

    def finish(r, carry):
        rows = pl.ds(pl.multiple_of(r * TR, TR), TR)
        for t in range(ct):
            cols = pl.ds(t * TC, TC)
            returned = back_recv[ret_ref[r * ct + t]]
            out_ref[rows, cols] = live_of(r, t) * (particle[rows, cols] - returned)
        return carry

    lax.fori_loop(0, rt, finish, 0)
    for copy in started:
        copy.wait_send()


def shards(
    generator,
    interaction,
    occupations,
    pair_orbits,
    cross_orbits,
    pair_sizes,
    cross_sizes,
    cross_target,
):
    height, width = generator.shape[1:]
    n_chan, n_col, n_sub = (lax.axis_size(axis) for axis in ("chan", "col", "sub"))
    rt, ct = height // TR, width // TC
    tiles = rt * ct
    cap = 2 * tiles // n_chan
    chunk = min(cap, 8)
    states = pair_orbits.shape[2]

    targets = cross_target[0].reshape(-1)
    owner = targets // tiles
    slot = targets % tiles
    index = jnp.arange(tiles, dtype=jnp.int32)
    same = (owner[:, None] == owner[None, :]) & (index[None, :] < index[:, None])
    rank = jnp.sum(same.astype(jnp.int32), axis=1)
    position = owner * cap + rank
    taken = position[None, :] == jnp.arange(n_chan * cap, dtype=jnp.int32)[:, None]
    pack_index = jnp.sum(jnp.where(taken, index[None, :], 0), axis=1)
    slot_map = jnp.sum(jnp.where(taken, slot[None, :], 0), axis=1)
    lands = targets[None, :] == jnp.arange(n_chan * tiles, dtype=jnp.int32)[:, None]
    label = lax.axis_index("chan") * cap + rank
    inverse = jnp.sum(jnp.where(lands, label[None, :], 0), axis=1)
    lanes = -(-(tiles + cap) // LANES) * LANES
    meta = jnp.concatenate(
        [
            inverse.reshape(n_chan, 1, tiles),
            slot_map.reshape(n_chan, 1, cap),
            jnp.zeros((n_chan, 1, lanes - tiles - cap), jnp.int32),
        ],
        axis=2,
    )
    sizes = jnp.stack([pair_sizes[0], cross_sizes[0]])
    filled = occupations.astype(jnp.float32)

    f32, bf16, i32 = jnp.float32, jnp.bfloat16, jnp.int32
    vmem = pl.BlockSpec(memory_space=pltpu.VMEM)
    smem = pl.BlockSpec(memory_space=pltpu.SMEM)
    dma = pltpu.SemaphoreType.DMA
    n_chunk = cap // chunk
    slots = n_chan * cap
    meta_row = (n_chan, 1, lanes)
    scratch = [
        pltpu.VMEM((tiles, TR, TC), f32),
        pltpu.VMEM((tiles, TR, TC), f32),
        pltpu.VMEM((slots - cap, TR, TC), f32),
        pltpu.VMEM((slots - cap, TR, TC), f32),
        pltpu.VMEM((slots, TR, TC), f32),
        pltpu.VMEM((slots, TR, TC), f32),
        pltpu.VMEM((n_col - 1, slots, TR, TC), f32),
        pltpu.VMEM((n_col - 1, slots, TR, TC), f32),
        pltpu.VMEM((n_sub - 1, slots, TR, TC), f32),
        pltpu.VMEM((n_sub - 1, slots, TR, TC), f32),
        pltpu.VMEM(meta_row, i32),
        pltpu.VMEM((n_col - 1,) + meta_row, i32),
        pltpu.VMEM((n_sub - 1,) + meta_row, i32),
        pltpu.SMEM(meta_row, i32),
        pltpu.SMEM((n_col - 1,) + meta_row, i32),
        pltpu.SMEM((n_sub - 1,) + meta_row, i32),
    ]
    scratch += [pltpu.VMEM((n_col, height, width), bf16)] * 4
    scratch += [pltpu.VMEM((n_sub * height, width), bf16)] * 4
    scratch += [
        pltpu.VMEM((tiles, TR, TC), f32),
        pltpu.VMEM((slots - cap, TR, TC), f32),
        pltpu.VMEM((slots, TR, TC), f32),
        pltpu.VMEM((2, n_col - 1, height, width), f32),
        pltpu.VMEM((2, n_sub - 1, height, width), f32),
        pltpu.VMEM((height, width), f32),
        pltpu.VMEM((2, states // TC, 8, TC), f32),
        dma((2, n_chunk, n_chan - 1)),
        dma((2, n_chunk, n_chan - 1)),
        dma((2, n_chunk, n_chan, n_col - 1)),
        dma((2, n_chunk, n_chan, n_col - 1)),
        dma((2, n_chunk, n_chan, n_sub - 1)),
        dma((2, n_chunk, n_chan, n_sub - 1)),
        dma((n_chan + n_col + n_sub - 3,)),
        dma((n_chan + n_col + n_sub - 3,)),
        dma((3,)),
        dma((n_chan - 1,)),
        dma((n_chan - 1,)),
        dma((2, n_col + n_sub - 2)),
        dma((2, n_col + n_sub - 2)),
    ]
    static = (n_chan, n_col, n_sub, height, width, cap, chunk)
    result = pl.pallas_call(
        functools.partial(kernel, static),
        out_shape=jax.ShapeDtypeStruct((height, width), f32),
        in_specs=[vmem, vmem, vmem, vmem, smem, smem, smem, smem, vmem],
        out_specs=vmem,
        scratch_shapes=scratch,
        compiler_params=pltpu.CompilerParams(
            collective_id=0, has_side_effects=True, vmem_limit_bytes=VMEM_LIMIT
        ),
        name="commutator",
    )(
        generator[0],
        interaction[0],
        pair_orbits[0],
        cross_orbits[0],
        filled,
        sizes,
        pack_index,
        position,
        meta,
    )
    return result[None]


def solution(mesh):
    return jax.shard_map(
        shards,
        mesh=mesh,
        in_specs=(
            P(("grp", "chan"), "sub", "col"),
            P(("grp", "chan"), "sub", "col"),
            P(),
            P("chan", None, None),
            P("chan", None, None),
            P("chan"),
            P("chan"),
            P("chan", "sub", "col"),
        ),
        out_specs=P(("grp", "chan"), "sub", "col"),
        check_vma=False,
    )
```

```python
import functools

import jax
import jax.numpy as jnp
from jax import lax
from jax.experimental import pallas as pl
from jax.experimental.pallas import tpu as pltpu
from jax.sharding import PartitionSpec as P

TR = 32
TC = 128
LANES = 128
MESH = pl.DeviceIdType.MESH
VMEM_LIMIT = 60 * 1024 * 1024
ROWS = 8
SLICES = TR // ROWS
LEAD = 2


def split(value):
    high = value.astype(jnp.bfloat16)
    low = (value - high.astype(jnp.float32)).astype(jnp.bfloat16)
    return high, low


def outer_first(count):
    order = []
    for edge in range((count + 1) // 2):
        order += [edge] if edge == count - 1 - edge else [edge, count - 1 - edge]
    return order, count // 2


def kernel(sizes, *refs):
    n_chan, n_col, n_sub, height, width, cap = sizes
    refs = list(refs)

    def grab(count):
        taken = refs[:count]
        del refs[:count]
        return taken

    gen_ref, int_ref, pair_orb_ref, cross_orb_ref, filled_ref = grab(5)
    size_ref, pack_ref, ret_ref, meta_ref, out_ref = grab(5)
    tiled = grab(2)
    sent = grab(2)
    raw = (grab(SLICES), grab(SLICES))
    whole = grab(2)
    from_col = grab(2)
    from_sub = grab(2)
    meta_own, smeta = grab(2)
    left = (grab(2), grab(2))
    right = (grab(2), grab(2))
    product, back_send, back_recv, partx, parts, particle, weights = grab(7)
    z_send, z_recv, x_send, x_recv, s_send, s_recv = grab(6)
    m_send, m_recv, local_sem, b_send, b_recv, p_send, p_recv = grab(7)

    rt, ct = height // TR, width // TC
    tiles = rt * ct
    me = lax.axis_index("chan")
    my_col = lax.axis_index("col")
    my_sub = lax.axis_index("sub")

    def to_col(step):
        return {"col": lax.rem(my_col + step, n_col)}

    def to_sub(step):
        return {"sub": lax.rem(my_sub + step, n_sub)}

    order, outer_count = outer_first(n_chan)
    upper = me // max(n_chan // 2, 1)
    peers = [upper * t + (1 - upper) * (n_chan - 1 - t) for t in order]

    barrier = pltpu.get_barrier_semaphore()
    for d in range(1, n_chan):
        pl.semaphore_signal(
            barrier, inc=1, device_id={"chan": lax.rem(me + d, n_chan)}, device_id_type=MESH
        )
    for d in range(1, n_col):
        pl.semaphore_signal(barrier, inc=1, device_id=to_col(d), device_id_type=MESH)
    for d in range(1, n_sub):
        pl.semaphore_signal(barrier, inc=1, device_id=to_sub(d), device_id_type=MESH)

    limit = size_ref[0]
    row_in = lax.broadcasted_iota(jnp.int32, (TR, TC), 0) + my_sub * height
    col_in = lax.broadcasted_iota(jnp.int32, (TR, TC), 1) + my_col * width

    def live_of(r, t):
        keep = (row_in + r * TR < limit) & (col_in + t * TC < limit)
        return keep.astype(jnp.float32)

    own_meta = pltpu.make_async_copy(meta_ref.at[me], meta_own.at[me], local_sem.at[0])
    own_meta.start()

    def to_tiles(r, carry):
        rows = pl.ds(pl.multiple_of(r * TR, TR), TR)
        for t in range(ct):
            keep = live_of(r, t)
            cols = pl.ds(t * TC, TC)
            tiled[0][r * ct + t] = gen_ref[rows, cols] * keep
            tiled[1][r * ct + t] = int_ref[rows, cols] * keep
        return carry

    lax.fori_loop(0, rt, to_tiles, 0)

    def pack_one(m):
        def put(k, carry):
            value = tiled[m][pack_ref[k]]
            for q in range(SLICES):
                sent[m][q, k] = value[q * ROWS : (q + 1) * ROWS]
            return carry

        lax.fori_loop(0, n_chan * cap, put, 0, unroll=8)

        def keep_own(k, carry):
            value = tiled[m][pack_ref[me * cap + k]]
            for q in range(SLICES):
                raw[m][q][me * cap + k] = value[q * ROWS : (q + 1) * ROWS]
            return carry

        lax.fori_loop(0, cap, keep_own, 0, unroll=min(cap, 4))

    pack_one(0)
    pl.semaphore_wait(barrier, n_chan + n_col + n_sub - 3)

    def remote(src, dst, ssem, rsem, device):
        return pltpu.make_async_remote_copy(
            src_ref=src,
            dst_ref=dst,
            send_sem=ssem,
            recv_sem=rsem,
            device_id=device,
            device_id_type=MESH,
        )

    def others(peer_list, act):
        for peer in peer_list:

            @pl.when(peer != me)
            def _(peer=peer):
                act(peer)

    def meta_copy(peer, source):
        return remote(
            meta_ref.at[peer],
            meta_own.at[source],
            m_send.at[peer],
            m_recv.at[source],
            {"chan": peer},
        )

    def z_copy(m, q, peer, source):
        return remote(
            sent[m].at[q, pl.ds(peer * cap, cap)],
            raw[m][q].at[pl.ds(source * cap, cap)],
            z_send.at[m, q, peer],
            z_recv.at[m, q, source],
            {"chan": peer},
        )

    def back_copy(peer, source):
        return remote(
            back_send.at[pl.ds(peer * cap, cap)],
            back_recv.at[pl.ds(source * cap, cap)],
            b_send.at[peer],
            b_recv.at[source],
            {"chan": peer},
        )

    stages = [(m, q) for m in range(2) for q in range(SLICES)]
    outer, inner = peers[:outer_count], peers[outer_count:]

    def send_steps(first, last):
        for step in range(first, last):
            if step < len(stages):
                others(outer, lambda p, s=stages[step]: z_copy(*s, p, me).start())
            if step >= LEAD:
                others(inner, lambda p, s=stages[step - LEAD]: z_copy(*s, p, me).start())

    others(peers, lambda p: meta_copy(p, me).start())
    send_steps(0, SLICES)

    started = []

    def start(copy):
        copy.start()
        started.append(copy)
        return copy

    p_copies = ([], [])

    def send_particle(m):
        ref = (gen_ref, int_ref)[m]
        for e in range(1, n_col):
            p_copies[m].append(
                start(
                    remote(
                        ref,
                        partx.at[m, e - 1],
                        p_send.at[m, e - 1],
                        p_recv.at[m, e - 1],
                        to_col(e),
                    )
                )
            )
        for e in range(1, n_sub):
            p_copies[m].append(
                start(
                    remote(
                        ref,
                        parts.at[m, e - 1],
                        p_send.at[m, n_col - 1 + e - 1],
                        p_recv.at[m, n_col - 1 + e - 1],
                        to_sub(e),
                    )
                )
            )

    send_particle(0)
    pack_one(1)
    send_steps(SLICES, len(stages) + LEAD)

    states = pair_orb_ref.shape[1]

    def look_up(orbit, found):
        value = filled_ref[orbit]
        pair_found, cross_found = found
        pair_found = pair_found + jnp.where(pair_orb_ref[...] == orbit, value, 0.0)
        cross_found = cross_found + jnp.where(cross_orb_ref[...] == orbit, value, 0.0)
        return pair_found, cross_found

    zero = jnp.zeros((2, states), jnp.float32)
    pair_found, cross_found = lax.fori_loop(0, filled_ref.shape[0], look_up, (zero, zero))
    state_id = lax.broadcasted_iota(jnp.int32, (1, states), 1)
    pair_weight = (1.0 - pair_found[0:1] - pair_found[1:2]) * (state_id < limit).astype(jnp.float32)
    cross_weight = (cross_found[0:1] - cross_found[1:2]) * (state_id < size_ref[1]).astype(
        jnp.float32
    )
    for g in range(states // TC):
        weights[0, g] = jnp.broadcast_to(pair_weight[:, g * TC : (g + 1) * TC], (8, TC))
        weights[1, g] = jnp.broadcast_to(cross_weight[:, g * TC : (g + 1) * TC], (8, TC))

    own_meta.wait()
    others(peers, lambda p: meta_copy(p, p).wait_recv())
    to_scalar = pltpu.make_async_copy(meta_own, smeta, local_sem.at[0])
    to_scalar.start()
    to_scalar.wait()

    x_copies, s_copies = {}, {}

    def take(m, q):
        others(peers, lambda p: z_copy(m, q, p, p).wait_recv())

        def one(j, carry):
            where = smeta[0, 0, j]
            for source in range(1, n_chan):
                where = where + smeta[source, 0, j]
            whole[m][q, j] = raw[m][q][where]
            return carry

        lax.fori_loop(0, tiles, one, 0, unroll=8)
        for e in range(1, n_col):
            x_copies[m, q, e] = start(
                remote(
                    whole[m].at[q],
                    from_col[m].at[e - 1, q],
                    x_send.at[m, q, e - 1],
                    x_recv.at[m, q, e - 1],
                    to_col(e),
                )
            )
        for e in range(1, n_sub):
            s_copies[m, q, e] = start(
                remote(
                    whole[m].at[q],
                    from_sub[m].at[e - 1, q],
                    s_send.at[m, q, e - 1],
                    s_recv.at[m, q, e - 1],
                    to_sub(e),
                )
            )

    def put_left(which, m, block, rows, t, value):
        weight = weights[which, block * ct + t][0:1]
        signed = value * (weight if m == 0 else -weight)
        high, low = split(signed)
        cols = pl.ds(t * TC, TC)
        left[m][0][block, rows, cols] = high
        left[m][1][block, rows, cols] = low

    def put_right(m, block, r, t, value):
        rows = pl.ds(pl.multiple_of(block * height + r * TR, TR), TR)
        high, low = split(value)
        cols = pl.ds(t * TC, TC)
        right[m][0][rows, cols] = high
        right[m][1][rows, cols] = low

    def place(which, m, read, in_left, in_right):
        def one_row(r, carry):
            rows = pl.ds(pl.multiple_of(r * TR, TR), TR)
            for t in range(ct):
                value = read(r, t, rows)
                if in_left is not None:
                    put_left(which, m, in_left, rows, t, value)
                if in_right is not None:
                    put_right(m, in_right, r, t, value)
            return carry

        lax.fori_loop(0, rt, one_row, 0)

    def joined(ref, r, t, *lead):
        parts_of = [ref[(*lead, q, r * ct + t)] for q in range(SLICES)]
        return jnp.concatenate(parts_of, axis=0)

    def col_block(e):
        return lax.rem(my_col + n_col - e, n_col)

    def sub_block(e):
        return lax.rem(my_sub + n_sub - e, n_sub)

    def settle(m):
        place(1, m, lambda r, t, rows: joined(whole[m], r, t), my_col, my_sub)
        for e in range(1, n_sub):
            for q in range(SLICES):
                s_copies[m, q, e].wait_recv()
            place(1, m, lambda r, t, rows: joined(from_sub[m], r, t, e - 1), None, sub_block(e))
        for e in range(1, n_col):
            for q in range(SLICES):
                x_copies[m, q, e].wait_recv()
            place(1, m, lambda r, t, rows: joined(from_col[m], r, t, e - 1), col_block(e), None)

    for q in range(SLICES):
        take(0, q)
    for q in range(SLICES - 1):
        take(1, q)
    settle(0)
    take(1, SLICES - 1)
    send_particle(1)
    settle(1)

    tall = min(256, height)
    wide = min(256, width)

    def multiply(write):
        def one(step, carry):
            rows = pl.ds(pl.multiple_of(step * tall, tall), tall)
            for c in range(width // wide):
                cols = pl.ds(c * wide, wide)
                total = None
                for k in range(n_col):
                    depth = pl.ds(k * width, width)
                    for m in range(2):
                        a_hi = left[m][0][k, rows, :]
                        a_lo = left[m][1][k, rows, :]
                        b_hi = right[1 - m][0][depth, cols]
                        b_lo = right[1 - m][1][depth, cols]
                        for a, b in ((a_hi, b_hi), (a_hi, b_lo), (a_lo, b_hi)):
                            term = jnp.dot(a, b, preferred_element_type=jnp.float32)
                            total = term if total is None else total + term
                write(step, rows, c, cols, total)
            return carry

        lax.fori_loop(0, height // tall, one, 0)

    def write_product(step, rows, c, cols, total):
        for r in range(tall // TR):
            for t in range(wide // TC):
                index = (step * (tall // TR) + r) * ct + c * (wide // TC) + t
                product[index] = total[r * TR : (r + 1) * TR, t * TC : (t + 1) * TC]

    multiply(write_product)

    def send_back(peer):
        def put_back(k, carry):
            back_send[peer * cap + k] = product[smeta[peer, 0, tiles + k]]
            return carry

        lax.fori_loop(0, cap, put_back, 0, unroll=min(cap, 8))

    others(peers, send_back)

    def keep_back(k, carry):
        back_recv[me * cap + k] = product[smeta[me, 0, tiles + k]]
        return carry

    lax.fori_loop(0, cap, keep_back, 0, unroll=min(cap, 8))
    others(peers, lambda p: back_copy(p, me).start())

    for m, ref in enumerate((gen_ref, int_ref)):
        place(
            0, m, lambda r, t, rows, ref=ref: ref[rows, pl.ds(t * TC, TC)], my_col, my_sub
        )
    for m in range(2):
        for copy in p_copies[m]:
            copy.wait_recv()
        for e in range(1, n_sub):
            place(
                0,
                m,
                lambda r, t, rows: parts[m, e - 1, rows, pl.ds(t * TC, TC)],
                None,
                sub_block(e),
            )
        for e in range(1, n_col):
            place(
                0,
                m,
                lambda r, t, rows: partx[m, e - 1, rows, pl.ds(t * TC, TC)],
                col_block(e),
                None,
            )

    def write_particle(step, rows, c, cols, total):
        particle[rows, cols] = total

    multiply(write_particle)
    others(peers, lambda p: back_copy(p, p).wait_recv())

    def finish(r, carry):
        rows = pl.ds(pl.multiple_of(r * TR, TR), TR)
        for t in range(ct):
            cols = pl.ds(t * TC, TC)
            returned = back_recv[ret_ref[r * ct + t]]
            out_ref[rows, cols] = live_of(r, t) * (particle[rows, cols] - returned)
        return carry

    lax.fori_loop(0, rt, finish, 0)
    others(peers, lambda p: meta_copy(p, me).wait_send())
    for m, q in stages:
        others(peers, lambda p: z_copy(m, q, p, me).wait_send())
    others(peers, lambda p: back_copy(p, me).wait_send())
    for copy in started:
        copy.wait_send()


def shards(
    generator,
    interaction,
    occupations,
    pair_orbits,
    cross_orbits,
    pair_sizes,
    cross_sizes,
    cross_target,
):
    height, width = generator.shape[1:]
    n_chan, n_col, n_sub = (lax.axis_size(axis) for axis in ("chan", "col", "sub"))
    rt, ct = height // TR, width // TC
    tiles = rt * ct
    cap = 2 * tiles // n_chan
    states = pair_orbits.shape[2]

    targets = cross_target[0].reshape(-1)
    owner = targets // tiles
    slot = targets % tiles
    index = jnp.arange(tiles, dtype=jnp.int32)
    same = (owner[:, None] == owner[None, :]) & (index[None, :] < index[:, None])
    rank = jnp.sum(same.astype(jnp.int32), axis=1)
    position = owner * cap + rank
    taken = position[None, :] == jnp.arange(n_chan * cap, dtype=jnp.int32)[:, None]
    pack_index = jnp.sum(jnp.where(taken, index[None, :], 0), axis=1)
    slot_map = jnp.sum(jnp.where(taken, slot[None, :], 0), axis=1)
    lands = targets[None, :] == jnp.arange(n_chan * tiles, dtype=jnp.int32)[:, None]
    label = lax.axis_index("chan") * cap + rank
    inverse = jnp.sum(jnp.where(lands, label[None, :], 0), axis=1)
    lanes = -(-(tiles + cap) // LANES) * LANES
    meta = jnp.concatenate(
        [
            inverse.reshape(n_chan, 1, tiles),
            slot_map.reshape(n_chan, 1, cap),
            jnp.zeros((n_chan, 1, lanes - tiles - cap), jnp.int32),
        ],
        axis=2,
    )
    sizes = jnp.stack([pair_sizes[0], cross_sizes[0]])
    filled = occupations.astype(jnp.float32)

    f32, bf16, i32 = jnp.float32, jnp.bfloat16, jnp.int32
    vmem = pl.BlockSpec(memory_space=pltpu.VMEM)
    smem = pl.BlockSpec(memory_space=pltpu.SMEM)
    dma = pltpu.SemaphoreType.DMA
    slots = n_chan * cap
    meta_row = (n_chan, 1, lanes)
    slice_of = (ROWS, TC)
    scratch = [pltpu.VMEM((tiles, TR, TC), f32)] * 2
    scratch += [pltpu.VMEM((SLICES, slots) + slice_of, f32)] * 2
    scratch += [pltpu.VMEM((slots,) + slice_of, f32)] * (2 * SLICES)
    scratch += [pltpu.VMEM((SLICES, tiles) + slice_of, f32)] * 2
    scratch += [pltpu.VMEM((n_col - 1, SLICES, tiles) + slice_of, f32)] * 2
    scratch += [pltpu.VMEM((n_sub - 1, SLICES, tiles) + slice_of, f32)] * 2
    scratch += [pltpu.VMEM(meta_row, i32), pltpu.SMEM(meta_row, i32)]
    scratch += [pltpu.VMEM((n_col, height, width), bf16)] * 4
    scratch += [pltpu.VMEM((n_sub * height, width), bf16)] * 4
    scratch += [
        pltpu.VMEM((tiles, TR, TC), f32),
        pltpu.VMEM((slots, TR, TC), f32),
        pltpu.VMEM((slots, TR, TC), f32),
        pltpu.VMEM((2, n_col - 1, height, width), f32),
        pltpu.VMEM((2, n_sub - 1, height, width), f32),
        pltpu.VMEM((height, width), f32),
        pltpu.VMEM((2, states // TC, 8, TC), f32),
    ]
    scratch += [dma((2, SLICES, n_chan))] * 2
    scratch += [dma((2, SLICES, n_col - 1))] * 2
    scratch += [dma((2, SLICES, n_sub - 1))] * 2
    scratch += [dma((n_chan,))] * 2
    scratch += [dma((1,))]
    scratch += [dma((n_chan,))] * 2
    scratch += [dma((2, n_col + n_sub - 2))] * 2
    static = (n_chan, n_col, n_sub, height, width, cap)
    result = pl.pallas_call(
        functools.partial(kernel, static),
        out_shape=jax.ShapeDtypeStruct((height, width), f32),
        in_specs=[vmem, vmem, vmem, vmem, smem, smem, smem, smem, vmem],
        out_specs=vmem,
        scratch_shapes=scratch,
        compiler_params=pltpu.CompilerParams(
            collective_id=0, has_side_effects=True, vmem_limit_bytes=VMEM_LIMIT
        ),
        name="commutator",
    )(
        generator[0],
        interaction[0],
        pair_orbits[0],
        cross_orbits[0],
        filled,
        sizes,
        pack_index,
        position,
        meta,
    )
    return result[None]


def solution(mesh):
    return jax.shard_map(
        shards,
        mesh=mesh,
        in_specs=(
            P(("grp", "chan"), "sub", "col"),
            P(("grp", "chan"), "sub", "col"),
            P(),
            P("chan", None, None),
            P("chan", None, None),
            P("chan"),
            P("chan"),
            P("chan", "sub", "col"),
        ),
        out_specs=P(("grp", "chan"), "sub", "col"),
        check_vma=False,
    )
```

```python
import functools

import jax
import jax.numpy as jnp
from jax import lax
from jax.experimental import pallas as pl
from jax.experimental.pallas import tpu as pltpu
from jax.sharding import PartitionSpec as P

TR = 32
TC = 128
LANES = 128
MESH = pl.DeviceIdType.MESH
VMEM_LIMIT = 44 * 1024 * 1024
ROWS = 8
SLICES = TR // ROWS
LEAD = 2


def split(value):
    high = value.astype(jnp.bfloat16)
    low = (value - high.astype(jnp.float32)).astype(jnp.bfloat16)
    return high, low


def outer_first(count):
    order = []
    for edge in range((count + 1) // 2):
        order += [edge] if edge == count - 1 - edge else [edge, count - 1 - edge]
    return order, count // 2


def kernel(sizes, *refs):
    n_chan, n_col, n_sub, height, width, cap = sizes
    refs = list(refs)

    def grab(count):
        taken = refs[:count]
        del refs[:count]
        return taken

    gen_ref, int_ref, pair_orb_ref, cross_orb_ref, filled_ref = grab(5)
    pair_size_ref, cross_size_ref, pack_ref, ret_ref, target_ref, out_ref = grab(6)
    tiled = grab(2)
    sent = grab(2)
    raw = (grab(SLICES), grab(SLICES))
    whole = grab(2)
    from_col = grab(2)
    from_sub = grab(2)
    meta_ref, meta_own, smeta = grab(3)
    left = (grab(2), grab(2))
    right = (grab(2), grab(2))
    product, back_send, back_recv, partx, parts, particle, weights = grab(7)
    z_send, z_recv, x_send, x_recv, s_send, s_recv = grab(6)
    m_send, m_recv, local_sem, b_send, b_recv, p_send, p_recv = grab(7)

    rt, ct = height // TR, width // TC
    tiles = rt * ct
    me = lax.axis_index("chan")
    my_col = lax.axis_index("col")
    my_sub = lax.axis_index("sub")

    def to_col(step):
        return {"col": lax.rem(my_col + step, n_col)}

    def to_sub(step):
        return {"sub": lax.rem(my_sub + step, n_sub)}

    order, outer_count = outer_first(n_chan)
    upper = me // max(n_chan // 2, 1)
    peers = [upper * t + (1 - upper) * (n_chan - 1 - t) for t in order]

    barrier = pltpu.get_barrier_semaphore()
    for d in range(1, n_chan):
        pl.semaphore_signal(
            barrier, inc=1, device_id={"chan": lax.rem(me + d, n_chan)}, device_id_type=MESH
        )
    for d in range(1, n_col):
        pl.semaphore_signal(barrier, inc=1, device_id=to_col(d), device_id_type=MESH)
    for d in range(1, n_sub):
        pl.semaphore_signal(barrier, inc=1, device_id=to_sub(d), device_id_type=MESH)

    limit = pair_size_ref[0]
    row_in = lax.broadcasted_iota(jnp.int32, (TR, TC), 0) + my_sub * height
    col_in = lax.broadcasted_iota(jnp.int32, (TR, TC), 1) + my_col * width

    def live_of(r, t):
        keep = (row_in + r * TR < limit) & (col_in + t * TC < limit)
        return keep.astype(jnp.float32)

    def to_tiles(r, carry):
        rows = pl.ds(pl.multiple_of(r * TR, TR), TR)
        for t in range(ct):
            keep = live_of(r, t)
            cols = pl.ds(t * TC, TC)
            tiled[0][r * ct + t] = gen_ref[rows, cols] * keep
            tiled[1][r * ct + t] = int_ref[rows, cols] * keep
        return carry

    lax.fori_loop(0, rt, to_tiles, 0)

    def pack_one(m):
        def put(k, carry):
            value = tiled[m][pack_ref[k]]
            for q in range(SLICES):
                sent[m][q, k] = value[q * ROWS : (q + 1) * ROWS]
            return carry

        lax.fori_loop(0, n_chan * cap, put, 0, unroll=8)

        def keep_own(k, carry):
            value = tiled[m][pack_ref[me * cap + k]]
            for q in range(SLICES):
                raw[m][q][me * cap + k] = value[q * ROWS : (q + 1) * ROWS]
            return carry

        lax.fori_loop(0, cap, keep_own, 0, unroll=min(cap, 4))

    meta_shape = (n_chan, meta_ref.shape[2])
    lane = lax.broadcasted_iota(jnp.int32, meta_shape, 1)
    to = lax.broadcasted_iota(jnp.int32, meta_shape, 0)
    land_id = jnp.where(lane < tiles, to * tiles + lane, -1)
    slot_id = jnp.where((lane >= tiles) & (lane < tiles + cap), to * cap + lane - tiles, -1)

    def fill_meta(i, rows):
        target, place_of = target_ref[i], ret_ref[i]
        owner = lax.div(target, tiles)
        rows = jnp.where(land_id == target, (me - owner) * cap + place_of, rows)
        return jnp.where(slot_id == place_of, target - owner * tiles, rows)

    meta_rows = lax.fori_loop(0, tiles, fill_meta, jnp.zeros(meta_shape, jnp.int32), unroll=4)
    for d in range(n_chan):
        meta_ref[d] = meta_rows[d : d + 1]
    pack_one(0)
    pl.semaphore_wait(barrier, n_chan + n_col + n_sub - 3)

    def remote(src, dst, ssem, rsem, device):
        return pltpu.make_async_remote_copy(
            src_ref=src,
            dst_ref=dst,
            send_sem=ssem,
            recv_sem=rsem,
            device_id=device,
            device_id_type=MESH,
        )

    def others(peer_list, act):
        for peer in peer_list:

            @pl.when(peer != me)
            def _(peer=peer):
                act(peer)

    def meta_copy(peer, source):
        return remote(
            meta_ref.at[peer],
            meta_own.at[source],
            m_send.at[peer],
            m_recv.at[source],
            {"chan": peer},
        )

    def z_copy(m, q, peer, source):
        return remote(
            sent[m].at[q, pl.ds(peer * cap, cap)],
            raw[m][q].at[pl.ds(source * cap, cap)],
            z_send.at[m, q, peer],
            z_recv.at[m, q, source],
            {"chan": peer},
        )

    def back_copy(peer, source):
        return remote(
            back_send.at[pl.ds(peer * cap, cap)],
            back_recv.at[pl.ds(source * cap, cap)],
            b_send.at[peer],
            b_recv.at[source],
            {"chan": peer},
        )

    stages = [(m, q) for m in range(2) for q in range(SLICES)]
    outer, inner = peers[:outer_count], peers[outer_count:]

    def send_steps(first, last):
        for step in range(first, last):
            if step < len(stages):
                others(outer, lambda p, s=stages[step]: z_copy(*s, p, me).start())
            if step >= LEAD:
                others(inner, lambda p, s=stages[step - LEAD]: z_copy(*s, p, me).start())

    own_meta = pltpu.make_async_copy(meta_ref.at[me], meta_own.at[me], local_sem.at[0])
    own_meta.start()
    others(peers, lambda p: meta_copy(p, me).start())
    send_steps(0, SLICES)

    started = []

    def start(copy):
        copy.start()
        started.append(copy)
        return copy

    p_copies = ([], [])

    def send_particle(m):
        ref = (gen_ref, int_ref)[m]
        for e in range(1, n_col):
            p_copies[m].append(
                start(
                    remote(
                        ref,
                        partx.at[m, e - 1],
                        p_send.at[m, e - 1],
                        p_recv.at[m, e - 1],
                        to_col(e),
                    )
                )
            )
        for e in range(1, n_sub):
            p_copies[m].append(
                start(
                    remote(
                        ref,
                        parts.at[m, e - 1],
                        p_send.at[m, n_col - 1 + e - 1],
                        p_recv.at[m, n_col - 1 + e - 1],
                        to_sub(e),
                    )
                )
            )

    send_particle(0)
    pack_one(1)
    send_steps(SLICES, len(stages) + LEAD)

    states = pair_orb_ref.shape[1]

    def look_up(orbit, found):
        value = filled_ref[orbit].astype(jnp.float32)
        pair_found, cross_found = found
        pair_found = pair_found + jnp.where(pair_orb_ref[...] == orbit, value, 0.0)
        cross_found = cross_found + jnp.where(cross_orb_ref[...] == orbit, value, 0.0)
        return pair_found, cross_found

    zero = jnp.zeros((2, states), jnp.float32)
    pair_found, cross_found = lax.fori_loop(0, filled_ref.shape[0], look_up, (zero, zero))
    state_id = lax.broadcasted_iota(jnp.int32, (1, states), 1)
    pair_weight = (1.0 - pair_found[0:1] - pair_found[1:2]) * (state_id < limit).astype(jnp.float32)
    cross_weight = (cross_found[0:1] - cross_found[1:2]) * (state_id < cross_size_ref[0]).astype(
        jnp.float32
    )
    for g in range(states // TC):
        weights[0, g] = jnp.broadcast_to(pair_weight[:, g * TC : (g + 1) * TC], (8, TC))
        weights[1, g] = jnp.broadcast_to(cross_weight[:, g * TC : (g + 1) * TC], (8, TC))

    own_meta.wait()
    others(peers, lambda p: meta_copy(p, p).wait_recv())
    to_scalar = pltpu.make_async_copy(meta_own, smeta, local_sem.at[0])
    to_scalar.start()
    to_scalar.wait()

    x_copies, s_copies = {}, {}

    def take(m, q):
        others(peers, lambda p: z_copy(m, q, p, p).wait_recv())

        def one(j, carry):
            where = smeta[0, 0, j]
            for source in range(1, n_chan):
                where = where + smeta[source, 0, j]
            whole[m][q, j] = raw[m][q][jnp.minimum(where, n_chan * cap - 1)]
            return carry

        lax.fori_loop(0, tiles, one, 0, unroll=8)
        for e in range(1, n_col):
            x_copies[m, q, e] = start(
                remote(
                    whole[m].at[q],
                    from_col[m].at[e - 1, q],
                    x_send.at[m, q, e - 1],
                    x_recv.at[m, q, e - 1],
                    to_col(e),
                )
            )
        for e in range(1, n_sub):
            s_copies[m, q, e] = start(
                remote(
                    whole[m].at[q],
                    from_sub[m].at[e - 1, q],
                    s_send.at[m, q, e - 1],
                    s_recv.at[m, q, e - 1],
                    to_sub(e),
                )
            )

    def put_left(which, m, block, rows, t, value):
        weight = weights[which, block * ct + t][0:1]
        signed = value * (weight if m == 0 else -weight)
        high, low = split(signed)
        cols = pl.ds(t * TC, TC)
        left[m][0][block, rows, cols] = high
        left[m][1][block, rows, cols] = low

    def put_right(m, block, r, t, value):
        rows = pl.ds(pl.multiple_of(block * height + r * TR, TR), TR)
        high, low = split(value)
        cols = pl.ds(t * TC, TC)
        right[m][0][rows, cols] = high
        right[m][1][rows, cols] = low

    def place(which, m, read, in_left, in_right):
        def one_row(r, carry):
            rows = pl.ds(pl.multiple_of(r * TR, TR), TR)
            for t in range(ct):
                value = read(r, t, rows)
                if in_left is not None:
                    put_left(which, m, in_left, rows, t, value)
                if in_right is not None:
                    put_right(m, in_right, r, t, value)
            return carry

        lax.fori_loop(0, rt, one_row, 0)

    def joined(ref, r, t, *lead):
        parts_of = [ref[(*lead, q, r * ct + t)] for q in range(SLICES)]
        return jnp.concatenate(parts_of, axis=0)

    def col_block(e):
        return lax.rem(my_col + n_col - e, n_col)

    def sub_block(e):
        return lax.rem(my_sub + n_sub - e, n_sub)

    def settle(m):
        place(1, m, lambda r, t, rows: joined(whole[m], r, t), my_col, my_sub)
        for e in range(1, n_sub):
            for q in range(SLICES):
                s_copies[m, q, e].wait_recv()
            place(1, m, lambda r, t, rows: joined(from_sub[m], r, t, e - 1), None, sub_block(e))
        for e in range(1, n_col):
            for q in range(SLICES):
                x_copies[m, q, e].wait_recv()
            place(1, m, lambda r, t, rows: joined(from_col[m], r, t, e - 1), col_block(e), None)

    for q in range(SLICES):
        take(0, q)
    for q in range(SLICES - 1):
        take(1, q)
    settle(0)
    take(1, SLICES - 1)
    send_particle(1)
    settle(1)

    tall = min(256, height)
    wide = min(256, width)

    def multiply(write):
        def one(step, carry):
            rows = pl.ds(pl.multiple_of(step * tall, tall), tall)
            for c in range(width // wide):
                cols = pl.ds(c * wide, wide)
                total = None
                for k in range(n_col):
                    depth = pl.ds(k * width, width)
                    for m in range(2):
                        a_hi = left[m][0][k, rows, :]
                        a_lo = left[m][1][k, rows, :]
                        b_hi = right[1 - m][0][depth, cols]
                        b_lo = right[1 - m][1][depth, cols]
                        for a, b in ((a_hi, b_hi), (a_hi, b_lo), (a_lo, b_hi)):
                            term = jnp.dot(a, b, preferred_element_type=jnp.float32)
                            total = term if total is None else total + term
                write(step, rows, c, cols, total)
            return carry

        lax.fori_loop(0, height // tall, one, 0)

    def write_product(step, rows, c, cols, total):
        for r in range(tall // TR):
            for t in range(wide // TC):
                index = (step * (tall // TR) + r) * ct + c * (wide // TC) + t
                product[index] = total[r * TR : (r + 1) * TR, t * TC : (t + 1) * TC]

    multiply(write_product)

    def send_back(peer):
        def put_back(k, carry):
            back_send[peer * cap + k] = product[smeta[peer, 0, tiles + k]]
            return carry

        lax.fori_loop(0, cap, put_back, 0, unroll=min(cap, 8))

    others(peers, send_back)

    def keep_back(k, carry):
        back_recv[me * cap + k] = product[smeta[me, 0, tiles + k]]
        return carry

    lax.fori_loop(0, cap, keep_back, 0, unroll=min(cap, 8))
    others(peers, lambda p: back_copy(p, me).start())

    for m, ref in enumerate((gen_ref, int_ref)):
        place(
            0, m, lambda r, t, rows, ref=ref: ref[rows, pl.ds(t * TC, TC)], my_col, my_sub
        )
    for m in range(2):
        for copy in p_copies[m]:
            copy.wait_recv()
        for e in range(1, n_sub):
            place(
                0,
                m,
                lambda r, t, rows: parts[m, e - 1, rows, pl.ds(t * TC, TC)],
                None,
                sub_block(e),
            )
        for e in range(1, n_col):
            place(
                0,
                m,
                lambda r, t, rows: partx[m, e - 1, rows, pl.ds(t * TC, TC)],
                col_block(e),
                None,
            )

    def write_particle(step, rows, c, cols, total):
        particle[rows, cols] = total

    multiply(write_particle)
    others(peers, lambda p: back_copy(p, p).wait_recv())

    def finish(r, carry):
        rows = pl.ds(pl.multiple_of(r * TR, TR), TR)
        for t in range(ct):
            cols = pl.ds(t * TC, TC)
            returned = back_recv[ret_ref[r * ct + t]]
            out_ref[rows, cols] = particle[rows, cols] - returned
        return carry

    lax.fori_loop(0, rt, finish, 0)
    others(peers, lambda p: meta_copy(p, me).wait_send())
    for m, q in stages:
        others(peers, lambda p: z_copy(m, q, p, me).wait_send())
    others(peers, lambda p: back_copy(p, me).wait_send())
    for copy in started:
        copy.wait_send()


def shards(
    generator,
    interaction,
    occupations,
    pair_orbits,
    cross_orbits,
    pair_sizes,
    cross_sizes,
    cross_target,
):
    height, width = generator.shape[1:]
    n_chan, n_col, n_sub = (lax.axis_size(axis) for axis in ("chan", "col", "sub"))
    rt, ct = height // TR, width // TC
    tiles = rt * ct
    cap = 2 * tiles // n_chan
    states = pair_orbits.shape[2]

    targets = cross_target[0].reshape(-1)
    owner = targets // tiles
    index = jnp.arange(tiles, dtype=jnp.int32)
    same = (owner[:, None] == owner[None, :]) & (index[None, :] < index[:, None])
    rank = jnp.sum(same.astype(jnp.int32), axis=1)
    position = owner * cap + rank
    taken = position[None, :] == jnp.arange(n_chan * cap, dtype=jnp.int32)[:, None]
    pack_index = jnp.sum(jnp.where(taken, index[None, :], 0), axis=1)
    lanes = -(-(tiles + cap) // LANES) * LANES
    f32, bf16, i32 = jnp.float32, jnp.bfloat16, jnp.int32
    vmem = pl.BlockSpec(memory_space=pltpu.VMEM)
    smem = pl.BlockSpec(memory_space=pltpu.SMEM)
    dma = pltpu.SemaphoreType.DMA
    slots = n_chan * cap
    meta_row = (n_chan, 1, lanes)
    slice_of = (ROWS, TC)
    scratch = [pltpu.VMEM((tiles, TR, TC), f32)] * 2
    scratch += [pltpu.VMEM((SLICES, slots) + slice_of, f32)] * 2
    scratch += [pltpu.VMEM((slots,) + slice_of, f32)] * (2 * SLICES)
    scratch += [pltpu.VMEM((SLICES, tiles) + slice_of, f32)] * 2
    scratch += [pltpu.VMEM((n_col - 1, SLICES, tiles) + slice_of, f32)] * 2
    scratch += [pltpu.VMEM((n_sub - 1, SLICES, tiles) + slice_of, f32)] * 2
    scratch += [pltpu.VMEM(meta_row, i32)] * 2 + [pltpu.SMEM(meta_row, i32)]
    scratch += [pltpu.VMEM((n_col, height, width), bf16)] * 4
    scratch += [pltpu.VMEM((n_sub * height, width), bf16)] * 4
    scratch += [
        pltpu.VMEM((tiles, TR, TC), f32),
        pltpu.VMEM((slots, TR, TC), f32),
        pltpu.VMEM((slots, TR, TC), f32),
        pltpu.VMEM((2, n_col - 1, height, width), f32),
        pltpu.VMEM((2, n_sub - 1, height, width), f32),
        pltpu.VMEM((height, width), f32),
        pltpu.VMEM((2, states // TC, 8, TC), f32),
    ]
    scratch += [dma((2, SLICES, n_chan))] * 2
    scratch += [dma((2, SLICES, n_col - 1))] * 2
    scratch += [dma((2, SLICES, n_sub - 1))] * 2
    scratch += [dma((n_chan,))] * 2
    scratch += [dma((1,))]
    scratch += [dma((n_chan,))] * 2
    scratch += [dma((2, n_col + n_sub - 2))] * 2
    static = (n_chan, n_col, n_sub, height, width, cap)
    result = pl.pallas_call(
        functools.partial(kernel, static),
        out_shape=jax.ShapeDtypeStruct((height, width), f32),
        in_specs=[vmem] * 4 + [smem] * 6,
        out_specs=vmem,
        scratch_shapes=scratch,
        compiler_params=pltpu.CompilerParams(
            collective_id=0, has_side_effects=True, vmem_limit_bytes=VMEM_LIMIT
        ),
        name="commutator",
    )(
        generator[0],
        interaction[0],
        pair_orbits[0],
        cross_orbits[0],
        occupations,
        pair_sizes,
        cross_sizes,
        pack_index,
        position,
        targets,
    )
    row_id = lax.axis_index("sub") * height + jnp.arange(height, dtype=jnp.int32)
    col_id = lax.axis_index("col") * width + jnp.arange(width, dtype=jnp.int32)
    live = (row_id < pair_sizes[0])[:, None] & (col_id < pair_sizes[0])[None, :]
    return (live.astype(f32) * result)[None]


def solution(mesh):
    return jax.shard_map(
        shards,
        mesh=mesh,
        in_specs=(
            P(("grp", "chan"), "sub", "col"),
            P(("grp", "chan"), "sub", "col"),
            P(),
            P("chan", None, None),
            P("chan", None, None),
            P("chan"),
            P("chan"),
            P("chan", "sub", "col"),
        ),
        out_specs=P(("grp", "chan"), "sub", "col"),
        check_vma=False,
    )
```

```python
import functools

import jax
import jax.numpy as jnp
from jax import lax
from jax.experimental import pallas as pl
from jax.experimental.pallas import tpu as pltpu
from jax.sharding import PartitionSpec as P

TR = 32
TC = 128
LANES = 128
MESH = pl.DeviceIdType.MESH
VMEM_LIMIT = 44 * 1024 * 1024
ROWS = 8
SLICES = TR // ROWS
LEAD = 2


def split(value):
    high = value.astype(jnp.bfloat16)
    low = (value - high.astype(jnp.float32)).astype(jnp.bfloat16)
    return high, low


def outer_first(count):
    order = []
    for edge in range((count + 1) // 2):
        order += [edge] if edge == count - 1 - edge else [edge, count - 1 - edge]
    return order, count // 2


def kernel(sizes, *refs):
    n_chan, n_col, n_sub, height, width, cap = sizes
    refs = list(refs)

    def grab(count):
        taken = refs[:count]
        del refs[:count]
        return taken

    gen_ref, int_ref, pair_orb_ref, cross_orb_ref, filled_ref = grab(5)
    pair_size_ref, cross_size_ref, pack_ref, ret_ref, target_ref, out_ref = grab(6)
    tiled = grab(2)
    sent = grab(2)
    raw = (grab(SLICES), grab(SLICES))
    whole = grab(2)
    from_col = grab(2)
    from_sub = grab(2)
    meta_ref, meta_own, smeta = grab(3)
    left = (grab(2), grab(2))
    right = (grab(2), grab(2))
    product, back_send, back_recv, partx, parts, particle, weights = grab(7)
    z_send, z_recv, x_send, x_recv, s_send, s_recv = grab(6)
    m_send, m_recv, local_sem, b_send, b_recv, p_send, p_recv = grab(7)

    rt, ct = height // TR, width // TC
    tiles = rt * ct
    me = lax.axis_index("chan")
    my_col = lax.axis_index("col")
    my_sub = lax.axis_index("sub")

    def to_col(step):
        return {"col": lax.rem(my_col + step, n_col)}

    def to_sub(step):
        return {"sub": lax.rem(my_sub + step, n_sub)}

    order, outer_count = outer_first(n_chan)
    upper = me // max(n_chan // 2, 1)
    peers = [upper * t + (1 - upper) * (n_chan - 1 - t) for t in order]

    barrier = pltpu.get_barrier_semaphore()
    for d in range(1, n_chan):
        pl.semaphore_signal(
            barrier, inc=1, device_id={"chan": lax.rem(me + d, n_chan)}, device_id_type=MESH
        )
    for d in range(1, n_col):
        pl.semaphore_signal(barrier, inc=1, device_id=to_col(d), device_id_type=MESH)
    for d in range(1, n_sub):
        pl.semaphore_signal(barrier, inc=1, device_id=to_sub(d), device_id_type=MESH)

    limit = pair_size_ref[0]
    row_in = lax.broadcasted_iota(jnp.int32, (TR, TC), 0) + my_sub * height
    col_in = lax.broadcasted_iota(jnp.int32, (TR, TC), 1) + my_col * width

    def live_of(r, t):
        keep = (row_in + r * TR < limit) & (col_in + t * TC < limit)
        return keep.astype(jnp.float32)

    def to_tiles(r, carry):
        rows = pl.ds(pl.multiple_of(r * TR, TR), TR)
        for t in range(ct):
            keep = live_of(r, t)
            cols = pl.ds(t * TC, TC)
            tiled[0][r * ct + t] = gen_ref[rows, cols] * keep
            tiled[1][r * ct + t] = int_ref[rows, cols] * keep
        return carry

    lax.fori_loop(0, rt, to_tiles, 0)

    def pack_one(m):
        def put(k, carry):
            value = tiled[m][pack_ref[k]]
            for q in range(SLICES):
                sent[m][q, k] = value[q * ROWS : (q + 1) * ROWS]
            return carry

        lax.fori_loop(0, n_chan * cap, put, 0, unroll=8)

        def keep_own(k, carry):
            value = tiled[m][pack_ref[me * cap + k]]
            for q in range(SLICES):
                raw[m][q][me * cap + k] = value[q * ROWS : (q + 1) * ROWS]
            return carry

        lax.fori_loop(0, cap, keep_own, 0, unroll=min(cap, 4))

    meta_shape = (n_chan, meta_ref.shape[2])
    lane = lax.broadcasted_iota(jnp.int32, meta_shape, 1)
    to = lax.broadcasted_iota(jnp.int32, meta_shape, 0)
    land_id = jnp.where(lane < tiles, to * tiles + lane, -1)
    slot_id = jnp.where((lane >= tiles) & (lane < tiles + cap), to * cap + lane - tiles, -1)

    def fill_meta(i, rows):
        target, place_of = target_ref[i], ret_ref[i]
        owner = lax.div(target, tiles)
        rows = jnp.where(land_id == target, (me - owner) * cap + place_of, rows)
        return jnp.where(slot_id == place_of, target - owner * tiles, rows)

    meta_rows = lax.fori_loop(0, tiles, fill_meta, jnp.zeros(meta_shape, jnp.int32), unroll=4)
    for d in range(n_chan):
        meta_ref[d] = meta_rows[d : d + 1]
    pack_one(0)
    pl.semaphore_wait(barrier, n_chan + n_col + n_sub - 3)

    def remote(src, dst, ssem, rsem, device):
        return pltpu.make_async_remote_copy(
            src_ref=src,
            dst_ref=dst,
            send_sem=ssem,
            recv_sem=rsem,
            device_id=device,
            device_id_type=MESH,
        )

    def others(peer_list, act):
        for peer in peer_list:

            @pl.when(peer != me)
            def _(peer=peer):
                act(peer)

    def meta_copy(peer, source):
        return remote(
            meta_ref.at[peer],
            meta_own.at[source],
            m_send.at[peer],
            m_recv.at[source],
            {"chan": peer},
        )

    def z_copy(m, q, peer, source):
        return remote(
            sent[m].at[q, pl.ds(peer * cap, cap)],
            raw[m][q].at[pl.ds(source * cap, cap)],
            z_send.at[m, q, peer],
            z_recv.at[m, q, source],
            {"chan": peer},
        )

    def back_copy(peer, source):
        return remote(
            back_send.at[pl.ds(peer * cap, cap)],
            back_recv.at[pl.ds(source * cap, cap)],
            b_send.at[peer],
            b_recv.at[source],
            {"chan": peer},
        )

    stages = [(m, q) for m in range(2) for q in range(SLICES)]
    outer, inner = peers[:outer_count], peers[outer_count:]

    def send_steps(first, last):
        for step in range(first, last):
            if step < len(stages):
                others(outer, lambda p, s=stages[step]: z_copy(*s, p, me).start())
            if step >= LEAD:
                others(inner, lambda p, s=stages[step - LEAD]: z_copy(*s, p, me).start())

    own_meta = pltpu.make_async_copy(meta_ref.at[me], meta_own.at[me], local_sem.at[0])
    own_meta.start()
    others(peers, lambda p: meta_copy(p, me).start())
    send_steps(0, SLICES)

    started = []

    def start(copy):
        copy.start()
        started.append(copy)
        return copy

    p_copies = ([], [])

    def send_particle(m):
        ref = (gen_ref, int_ref)[m]
        for e in range(1, n_col):
            p_copies[m].append(
                start(
                    remote(
                        ref,
                        partx.at[m, e - 1],
                        p_send.at[m, e - 1],
                        p_recv.at[m, e - 1],
                        to_col(e),
                    )
                )
            )
        for e in range(1, n_sub):
            p_copies[m].append(
                start(
                    remote(
                        ref,
                        parts.at[m, e - 1],
                        p_send.at[m, n_col - 1 + e - 1],
                        p_recv.at[m, n_col - 1 + e - 1],
                        to_sub(e),
                    )
                )
            )

    send_particle(0)
    pack_one(1)
    send_steps(SLICES, len(stages) + LEAD)

    states = pair_orb_ref.shape[1]

    def look_up(orbit, found):
        value = filled_ref[orbit].astype(jnp.float32)
        pair_found, cross_found = found
        pair_found = pair_found + jnp.where(pair_orb_ref[...] == orbit, value, 0.0)
        cross_found = cross_found + jnp.where(cross_orb_ref[...] == orbit, value, 0.0)
        return pair_found, cross_found

    zero = jnp.zeros((2, states), jnp.float32)
    pair_found, cross_found = lax.fori_loop(0, filled_ref.shape[0], look_up, (zero, zero))
    state_id = lax.broadcasted_iota(jnp.int32, (1, states), 1)
    pair_weight = (1.0 - pair_found[0:1] - pair_found[1:2]) * (state_id < limit).astype(jnp.float32)
    cross_weight = (cross_found[0:1] - cross_found[1:2]) * (state_id < cross_size_ref[0]).astype(
        jnp.float32
    )
    for g in range(states // TC):
        weights[0, g] = jnp.broadcast_to(pair_weight[:, g * TC : (g + 1) * TC], (8, TC))
        weights[1, g] = jnp.broadcast_to(cross_weight[:, g * TC : (g + 1) * TC], (8, TC))

    own_meta.wait()
    others(peers, lambda p: meta_copy(p, p).wait_recv())
    to_scalar = pltpu.make_async_copy(meta_own, smeta, local_sem.at[0])
    to_scalar.start()
    to_scalar.wait()

    x_copies, s_copies = {}, {}

    def take(m, q):
        others(peers, lambda p: z_copy(m, q, p, p).wait_recv())

        def one(j, carry):
            where = smeta[0, 0, j]
            for source in range(1, n_chan):
                where = where + smeta[source, 0, j]
            whole[m][q, j] = raw[m][q][jnp.minimum(where, n_chan * cap - 1)]
            return carry

        lax.fori_loop(0, tiles, one, 0, unroll=8)
        for e in range(1, n_col):
            x_copies[m, q, e] = start(
                remote(
                    whole[m].at[q],
                    from_col[m].at[e - 1, q],
                    x_send.at[m, q, e - 1],
                    x_recv.at[m, q, e - 1],
                    to_col(e),
                )
            )
        for e in range(1, n_sub):
            s_copies[m, q, e] = start(
                remote(
                    whole[m].at[q],
                    from_sub[m].at[e - 1, q],
                    s_send.at[m, q, e - 1],
                    s_recv.at[m, q, e - 1],
                    to_sub(e),
                )
            )

    def put_left(which, m, block, rows, t, value):
        weight = weights[which, block * ct + t][0:1]
        signed = value * (weight if m == 0 else -weight)
        high, low = split(signed)
        cols = pl.ds(t * TC, TC)
        left[m][0][block, rows, cols] = high
        left[m][1][block, rows, cols] = low

    def put_right(m, block, r, t, value):
        rows = pl.ds(pl.multiple_of(block * height + r * TR, TR), TR)
        high, low = split(value)
        cols = pl.ds(t * TC, TC)
        right[m][0][rows, cols] = high
        right[m][1][rows, cols] = low

    def place(which, m, read, in_left, in_right):
        def one_row(r, carry):
            rows = pl.ds(pl.multiple_of(r * TR, TR), TR)
            for t in range(ct):
                value = read(r, t, rows)
                if in_left is not None:
                    put_left(which, m, in_left, rows, t, value)
                if in_right is not None:
                    put_right(m, in_right, r, t, value)
            return carry

        lax.fori_loop(0, rt, one_row, 0)

    def joined(ref, r, t, *lead):
        parts_of = [ref[(*lead, q, r * ct + t)] for q in range(SLICES)]
        return jnp.concatenate(parts_of, axis=0)

    def col_block(e):
        return lax.rem(my_col + n_col - e, n_col)

    def sub_block(e):
        return lax.rem(my_sub + n_sub - e, n_sub)

    def settle(m):
        place(1, m, lambda r, t, rows: joined(whole[m], r, t), my_col, my_sub)
        for e in range(1, n_sub):
            for q in range(SLICES):
                s_copies[m, q, e].wait_recv()
            place(1, m, lambda r, t, rows: joined(from_sub[m], r, t, e - 1), None, sub_block(e))
        for e in range(1, n_col):
            for q in range(SLICES):
                x_copies[m, q, e].wait_recv()
            place(1, m, lambda r, t, rows: joined(from_col[m], r, t, e - 1), col_block(e), None)

    for q in range(SLICES):
        take(0, q)
    for q in range(SLICES - 1):
        take(1, q)
    settle(0)
    take(1, SLICES - 1)
    send_particle(1)
    settle(1)

    tall = min(256, height)
    wide = min(256, width)

    def multiply(write):
        def one(step, carry):
            rows = pl.ds(pl.multiple_of(step * tall, tall), tall)
            for c in range(width // wide):
                cols = pl.ds(c * wide, wide)
                total = None
                for k in range(n_col):
                    depth = pl.ds(k * width, width)
                    for m in range(2):
                        a_hi = left[m][0][k, rows, :]
                        a_lo = left[m][1][k, rows, :]
                        b_hi = right[1 - m][0][depth, cols]
                        b_lo = right[1 - m][1][depth, cols]
                        for a, b in ((a_hi, b_hi), (a_hi, b_lo), (a_lo, b_hi)):
                            term = jnp.dot(a, b, preferred_element_type=jnp.float32)
                            total = term if total is None else total + term
                write(step, rows, c, cols, total)
            return carry

        lax.fori_loop(0, height // tall, one, 0)

    def write_product(step, rows, c, cols, total):
        for r in range(tall // TR):
            for t in range(wide // TC):
                index = (step * (tall // TR) + r) * ct + c * (wide // TC) + t
                product[index] = total[r * TR : (r + 1) * TR, t * TC : (t + 1) * TC]

    multiply(write_product)

    def send_back(peer):
        def put_back(k, carry):
            back_send[peer * cap + k] = product[smeta[peer, 0, tiles + k]]
            return carry

        lax.fori_loop(0, cap, put_back, 0, unroll=min(cap, 8))

    others(peers, send_back)

    others(peers, lambda p: back_copy(p, me).start())

    def keep_back(k, carry):
        back_recv[me * cap + k] = product[smeta[me, 0, tiles + k]]
        return carry

    lax.fori_loop(0, cap, keep_back, 0, unroll=min(cap, 8))

    for m, ref in enumerate((gen_ref, int_ref)):
        place(
            0, m, lambda r, t, rows, ref=ref: ref[rows, pl.ds(t * TC, TC)], my_col, my_sub
        )
    for m in range(2):
        for copy in p_copies[m]:
            copy.wait_recv()
        for e in range(1, n_sub):
            place(
                0,
                m,
                lambda r, t, rows: parts[m, e - 1, rows, pl.ds(t * TC, TC)],
                None,
                sub_block(e),
            )
        for e in range(1, n_col):
            place(
                0,
                m,
                lambda r, t, rows: partx[m, e - 1, rows, pl.ds(t * TC, TC)],
                col_block(e),
                None,
            )

    def write_particle(step, rows, c, cols, total):
        particle[rows, cols] = total

    multiply(write_particle)
    others(peers, lambda p: back_copy(p, p).wait_recv())

    def finish(r, carry):
        rows = pl.ds(pl.multiple_of(r * TR, TR), TR)
        for t in range(ct):
            cols = pl.ds(t * TC, TC)
            returned = back_recv[ret_ref[r * ct + t]]
            out_ref[rows, cols] = particle[rows, cols] - returned
        return carry

    lax.fori_loop(0, rt, finish, 0)
    others(peers, lambda p: meta_copy(p, me).wait_send())
    for m, q in stages:
        others(peers, lambda p: z_copy(m, q, p, me).wait_send())
    others(peers, lambda p: back_copy(p, me).wait_send())
    for copy in started:
        copy.wait_send()


def shards(
    generator,
    interaction,
    occupations,
    pair_orbits,
    cross_orbits,
    pair_sizes,
    cross_sizes,
    cross_target,
):
    height, width = generator.shape[1:]
    n_chan, n_col, n_sub = (lax.axis_size(axis) for axis in ("chan", "col", "sub"))
    rt, ct = height // TR, width // TC
    tiles = rt * ct
    cap = 2 * tiles // n_chan
    states = pair_orbits.shape[2]

    targets = cross_target[0].reshape(-1)
    owner = targets // tiles
    index = jnp.arange(tiles, dtype=jnp.int32)
    same = (owner[:, None] == owner[None, :]) & (index[None, :] < index[:, None])
    rank = jnp.sum(same.astype(jnp.int32), axis=1)
    position = owner * cap + rank
    taken = position[None, :] == jnp.arange(n_chan * cap, dtype=jnp.int32)[:, None]
    pack_index = jnp.sum(jnp.where(taken, index[None, :], 0), axis=1)
    lanes = -(-(tiles + cap) // LANES) * LANES
    f32, bf16, i32 = jnp.float32, jnp.bfloat16, jnp.int32
    vmem = pl.BlockSpec(memory_space=pltpu.VMEM)
    smem = pl.BlockSpec(memory_space=pltpu.SMEM)
    dma = pltpu.SemaphoreType.DMA
    slots = n_chan * cap
    meta_row = (n_chan, 1, lanes)
    slice_of = (ROWS, TC)
    scratch = [pltpu.VMEM((tiles, TR, TC), f32)] * 2
    scratch += [pltpu.VMEM((SLICES, slots) + slice_of, f32)] * 2
    scratch += [pltpu.VMEM((slots,) + slice_of, f32)] * (2 * SLICES)
    scratch += [pltpu.VMEM((SLICES, tiles) + slice_of, f32)] * 2
    scratch += [pltpu.VMEM((n_col - 1, SLICES, tiles) + slice_of, f32)] * 2
    scratch += [pltpu.VMEM((n_sub - 1, SLICES, tiles) + slice_of, f32)] * 2
    scratch += [pltpu.VMEM(meta_row, i32)] * 2 + [pltpu.SMEM(meta_row, i32)]
    scratch += [pltpu.VMEM((n_col, height, width), bf16)] * 4
    scratch += [pltpu.VMEM((n_sub * height, width), bf16)] * 4
    scratch += [
        pltpu.VMEM((tiles, TR, TC), f32),
        pltpu.VMEM((slots, TR, TC), f32),
        pltpu.VMEM((slots, TR, TC), f32),
        pltpu.VMEM((2, n_col - 1, height, width), f32),
        pltpu.VMEM((2, n_sub - 1, height, width), f32),
        pltpu.VMEM((height, width), f32),
        pltpu.VMEM((2, states // TC, 8, TC), f32),
    ]
    scratch += [dma((2, SLICES, n_chan))] * 2
    scratch += [dma((2, SLICES, n_col - 1))] * 2
    scratch += [dma((2, SLICES, n_sub - 1))] * 2
    scratch += [dma((n_chan,))] * 2
    scratch += [dma((1,))]
    scratch += [dma((n_chan,))] * 2
    scratch += [dma((2, n_col + n_sub - 2))] * 2
    static = (n_chan, n_col, n_sub, height, width, cap)
    result = pl.pallas_call(
        functools.partial(kernel, static),
        out_shape=jax.ShapeDtypeStruct((height, width), f32),
        in_specs=[vmem] * 4 + [smem] * 6,
        out_specs=vmem,
        scratch_shapes=scratch,
        compiler_params=pltpu.CompilerParams(
            collective_id=0, has_side_effects=True, vmem_limit_bytes=VMEM_LIMIT
        ),
        name="commutator",
    )(
        generator[0],
        interaction[0],
        pair_orbits[0],
        cross_orbits[0],
        occupations,
        pair_sizes,
        cross_sizes,
        pack_index,
        position,
        targets,
    )
    row_id = lax.axis_index("sub") * height + jnp.arange(height, dtype=jnp.int32)
    col_id = lax.axis_index("col") * width + jnp.arange(width, dtype=jnp.int32)
    live = (row_id < pair_sizes[0])[:, None] & (col_id < pair_sizes[0])[None, :]
    return (live.astype(f32) * result)[None]


def solution(mesh):
    return jax.shard_map(
        shards,
        mesh=mesh,
        in_specs=(
            P(("grp", "chan"), "sub", "col"),
            P(("grp", "chan"), "sub", "col"),
            P(),
            P("chan", None, None),
            P("chan", None, None),
            P("chan"),
            P("chan"),
            P("chan", "sub", "col"),
        ),
        out_specs=P(("grp", "chan"), "sub", "col"),
        check_vma=False,
    )
```
